32 devices in a mesh: parts: 2 (over y), seq: 4 (over z), chan: 4 (over x, core).
Axes of the slice: x: 2, y: 2, z: 4, core: 2. Of those that a mesh axis runs over, the one named last changes fastest.
Arguments:
- x_tokens: bfloat16 [64, 8192], P(('parts', 'seq'), 'chan'), parts along dimension 0, may hold values from -6 to 6
- norm_gain: float32 [8192], P('chan'), may hold values from 0.5 to 1.5
- w_in: bfloat16 [3, 8192, 8192], P(None, 'seq', 'chan'), may hold values from -0.0625 to 0.0625
- short_filter: float32 [3, 3, 8192], P(None, None, 'seq'), may hold values from -3 to 3
- se_filter: float32 [7, 512], P(None, 'seq'), may hold values from -2 to 2
- w_out: bfloat16 [8192, 8192], P('seq'), may hold values from -0.0625 to 0.0625
Outputs:
- mixed_out: bfloat16 [64, 8192], P(('parts', 'chan'), 'seq'), parts along dimension 0
The draws below stay inside these ranges and needn't reach their ends.
There are 2 independent parts, one for each index of `parts`. The reference program is written for one: setup_inputs(seed, part) draws one part's arguments, and reference() takes and returns one part's arrays. A program takes and returns all parts, laid end to end along the dimension named above; an argument that names none is the same for every part. Nothing has to cross between parts.
All inputs are finite; a program needn't handle non-finite values.
Results may differ from the reference program's by a relative error of at most 0.0086.
Values may be sent and summed in bfloat16 or wider, within the bound.
No kernel may reach another device: no remote copies, remote signals or barrier semaphores. Data moves between devices by JAX's collectives and lax.ppermute only.
A program may use at most 128 MiB of HBM per device.

```python
import jax
import jax.numpy as jnp
from jax import lax

D = 8192
GROUP = 16
TOKENS = 32
FILTERS = 512


def block_levels(stream_key, extent, shards, smallest, top_value):
    def one(dim, shards_of):
        draws = jax.random.uniform(jax.random.fold_in(jax.random.fold_in(stream_key, 6), dim), (shards_of,), jnp.float32, smallest / len(shards), top_value / len(shards))
        return jnp.repeat(jnp.exp(draws), extent[dim] // shards_of).reshape((-1,) + (1,) * (len(extent) - dim - 1))

    loudness = one(*shards[0])
    for cut in shards[1:]:
        loudness = loudness * one(*cut)
    return loudness


def noise(key, extent, spread, bound, pieces=(), dtype=jnp.bfloat16):
    values = jax.random.normal(key, extent, jnp.float32) * spread
    if len(pieces) > 0:
        values = block_levels(key, extent, pieces, -0.22, 0.18) * values
    return jnp.clip(values, min=-bound, max=bound).astype(dtype)


def setup_inputs(seed: int = 0, part: int = 0) -> dict:
    seeds = jax.random.split(jax.random.key(seed), 7)
    own_keys = jax.random.split(jax.random.fold_in(seeds[6], part), 7)
    x_tokens = noise(own_keys[0], (TOKENS, D), 1.0, 6.0, ((0, 4), (1, 4)))
    norm_gain = jnp.clip(1.0 + 0.1 * jax.random.normal(seeds[1], (D,), jnp.float32), 0.5, 1.5)
    w_in = noise(seeds[2], (3, D, D), D ** -0.5, 0.0625, ((1, 4), (2, 4)))
    short_filter = noise(seeds[3], (3, 3, D), 0.6, 3.0, ((2, 4),), jnp.float32)
    se_filter = noise(seeds[4], (7, FILTERS), 0.4, 2.0, ((1, 4),), jnp.float32)
    w_out = noise(seeds[5], (D, D), D ** -0.5, 0.0625, ((0, 4),))
    return {"x_tokens": x_tokens, "norm_gain": norm_gain, "w_in": w_in, "short_filter": short_filter, "se_filter": se_filter, "w_out": w_out}


epsilon = 1e-06

def rms_normalize(rows, gain):
    wide = rows.astype(jnp.float32)
    factor = lax.rsqrt(lax.optimization_barrier(jnp.mean(wide * wide, axis=-1, keepdims=True)) + epsilon)
    return (wide * factor * gain).astype(jnp.bfloat16)

def mixer(extended, short_taps, long_taps):
    wide = extended.astype(jnp.float32)
    row_count = wide.shape[0]
    featured = sum((short_taps[offset] * wide[2 - offset:row_count - offset] for offset in range(3)))
    queries = featured[:, 0]
    product = featured[:, 1] * featured[:, 2]
    length = product.shape[0]
    filtered = sum((long_taps[offset] * product[6 - offset:length - offset] for offset in range(7)))
    return (queries[6:] * filtered).astype(jnp.bfloat16)

def reference(x_tokens, norm_gain, w_in, short_filter, se_filter, w_out):
    normed = rms_normalize(x_tokens, norm_gain)
    flat_in = w_in.reshape(3 * D, D)
    projected = lax.dot_general(normed, flat_in, (((1,), (1,)), ((), ())), preferred_element_type=jnp.float32).astype(jnp.bfloat16)
    projected = projected.reshape(TOKENS, 3, D)
    extended = jnp.concatenate([jnp.zeros((8, 3, D), jnp.bfloat16), projected], axis=0)
    gated = mixer(extended, short_filter, jnp.repeat(se_filter, GROUP, axis=1))
    mixed = lax.dot_general(gated, w_out, (((1,), (1,)), ((), ())), preferred_element_type=jnp.float32)
    return mixed.astype(jnp.bfloat16)
```

```python
import functools

import jax
import jax.numpy as jnp
from jax import lax
from jax.experimental import pallas as pl
from jax.experimental.pallas import tpu as pltpu
from jax.sharding import PartitionSpec as P

GROUP = 16
epsilon = 1e-06
LANES = 128
PACK = 4
VMEM = pl.BlockSpec(memory_space=pltpu.VMEM)
ANY = pl.BlockSpec(memory_space=pl.ANY)
F32, BF16 = jnp.float32, jnp.bfloat16


def contract_last(left, right):
    return lax.dot_general(left, right, (((1,), (1,)), ((), ())), preferred_element_type=F32)


def spread(rows):
    blank = jnp.zeros_like(rows)
    return [jnp.concatenate([rows if i == q else blank for i in range(PACK)], axis=0) for q in range(PACK)]


def call(body, outs, ins, scratch=(), limit=2, cost=None):
    return pl.pallas_call(
        body,
        out_shape=outs,
        in_specs=ins,
        out_specs=jax.tree.map(lambda _: VMEM, outs),
        scratch_shapes=list(scratch),
        compiler_params=pltpu.CompilerParams(vmem_limit_bytes=limit << 20),
        cost_estimate=cost,
    )


def struct(shape, dtype):
    return jax.ShapeDtypeStruct(shape, dtype)


def open_body(x_ref, o_ref):
    o_ref[...] = x_ref[...]


def taps_body(se, out):
    groups, quarter = se.shape[1], out.shape[1]
    first = lax.axis_index("chan") * (quarter // GROUP)
    row = lax.broadcasted_iota(jnp.int32, (groups, quarter), 0)
    column = lax.broadcasted_iota(jnp.int32, (groups, quarter), 1)
    chosen = jnp.where(row == first + column // GROUP, 1.0, 0.0).astype(BF16)
    rest, total = se[...], 0.0
    for _ in range(3):
        part = rest.astype(BF16)
        total = total + jnp.dot(part, chosen, preferred_element_type=F32)
        rest = rest - part.astype(F32)
    out[...] = total


def high_low(squares):
    high = squares.astype(BF16).astype(F32)
    low = (squares - high).astype(BF16).astype(F32)
    lane = lax.broadcasted_iota(jnp.int32, (8, LANES), 1)
    count = squares.shape[0] // 8
    return jnp.concatenate(
        [jnp.where(lane < LANES // 2, high[8 * i : 8 * i + 8], low[8 * i : 8 * i + 8]) for i in range(count)], axis=1
    )


def from_high_low(packed, count):
    return jnp.concatenate(
        [packed[:, i * LANES : i * LANES + 1] + packed[:, i * LANES + LANES // 2 : i * LANES + LANES // 2 + 1] for i in range(count)],
        axis=0,
    )


def project_body(seq, quarter, *refs):
    pieces, (gain, w_in), (send, keep), (wide,) = refs[:seq], refs[seq : seq + 2], refs[seq + 2 : seq + 4], refs[seq + 4 :]
    s, c = lax.axis_index("seq"), lax.axis_index("chan")
    rows = pieces[0].shape[0]
    for hop in range(seq):
        place = pl.multiple_of(jnp.bitwise_xor(s, hop) * rows, rows)
        wide[pl.ds(place, rows), :] = pieces[hop][...].astype(F32)
    tokens = wide[...]
    squares = jnp.sum(tokens * tokens, axis=1, keepdims=True)
    packs = spread((tokens * gain[...]).astype(BF16))
    count = tokens.shape[0]
    half = quarter // 2
    for other in (1, 0):
        for comp in range(3):
            total = None
            for chip in range(2):
                owner = jnp.bitwise_xor(c, 2 * chip + other)
                for h in range(2):
                    start = pl.multiple_of(owner * quarter + h * half, half)
                    term = contract_last(w_in[comp, pl.ds(start, half), :], packs[2 * chip + h])
                    total = term if total is None else total + term
            flipped = total.T
            for chip in range(2):
                value = flipped[2 * chip * count : 2 * (chip + 1) * count]
                if other:
                    send[chip, : 2 * count, comp * half : (comp + 1) * half] = value.astype(BF16)
                else:
                    keep[chip, : 2 * count, comp * half : (comp + 1) * half] = value
    packed = high_low(squares)
    width = packed.shape[1]
    for chip in range(2):
        keep[chip, 2 * count :, :width] = packed
        send[chip, 2 * count :, :width] = packed.astype(BF16)
        keep[chip, 2 * count :, width:] = jnp.zeros((8, 3 * half - width), F32)
        send[chip, 2 * count :, width:] = jnp.zeros((8, 3 * half - width), BF16)


def relay_body(rows, keep, got, out):
    value = keep[1] + got[1].astype(F32)
    out[:rows, :] = value[:rows].astype(BF16)
    count = rows // 16
    width = count * LANES
    packed = high_low(from_high_low(value[rows:], count))
    out[rows:, :width] = packed.astype(BF16)
    out[rows:, width:] = jnp.zeros((8, value.shape[1] - width), BF16)


def later(value, lag):
    if lag == 0:
        return value
    return jnp.concatenate([jnp.zeros((lag, value.shape[1]), value.dtype), value[: value.shape[0] - lag]], axis=0)


def mix_body(features, keep, near, far, short, long_ref, out):
    c = lax.axis_index("chan")
    value = keep[0] + near[0].astype(F32) + far[...].astype(F32)
    rows = value.shape[0] - 8
    count = rows // 2
    half = value.shape[1] // 3
    squares = from_high_low(value[rows:], count // 8)
    factor = lax.rsqrt(squares / features + epsilon)
    for h in range(2):
        scaled = value[h * count : (h + 1) * count] * factor
        start = pl.multiple_of(c * (2 * half) + h * half, LANES)
        featured = []
        for comp in range(3):
            part = scaled[:, comp * half : (comp + 1) * half]
            taps = [short[lag, comp : comp + 1, pl.ds(start, half)] for lag in range(3)]
            featured.append(sum(taps[lag] * later(part, lag) for lag in range(3)))
        product = featured[1] * featured[2]
        filtered = sum(
            long_ref[lag : lag + 1, h * half : (h + 1) * half] * later(product, lag) for lag in range(long_ref.shape[0])
        )
        out[:, h * half : (h + 1) * half] = (featured[0] * filtered).astype(BF16)


def output_body(seq, quarter, *refs):
    pieces, w_out, (send, keep), (wide,) = refs[:seq], refs[seq], refs[seq + 1 : seq + 3], refs[seq + 3 :]
    s, c = lax.axis_index("seq"), lax.axis_index("chan")
    outputs = w_out.shape[0]
    block = w_out.shape[1] // seq
    part = outputs // PACK
    count = pieces[0].shape[0]
    total = None
    for hop in range(seq):
        source = jnp.bitwise_xor(s, hop)
        start = pl.multiple_of(source * block + c * quarter, LANES)
        packs = spread(pieces[hop][...])
        for q in range(PACK):
            term = contract_last(w_out[q * part : (q + 1) * part, pl.ds(start, quarter)], packs[q])
            total = term if total is None else total + term
    flipped = total.T
    for q in range(PACK):
        wide[:, q * part : (q + 1) * part] = flipped[q * count : (q + 1) * count]
    rows = send.shape[1]
    for chip in range(2):
        for other in range(2):
            owner = jnp.bitwise_xor(c, 2 * chip + other)
            value = wide[pl.ds(pl.multiple_of(owner * rows, rows), rows), :]
            if other:
                send[chip] = value.astype(BF16)
            else:
                keep[chip] = value


def pass_body(keep, got, out):
    out[...] = (keep[1] + got[1].astype(F32)).astype(BF16)


def close_body(keep, near, far, out):
    out[...] = (keep[0] + near[0].astype(F32) + far[...].astype(F32)).astype(BF16)


def swap(value, axis, bit):
    return lax.ppermute(value, axis, [(i, i ^ bit) for i in range(lax.axis_size(axis))])


def gathered(value, axis):
    return [value] + [swap(value, axis, bit) for bit in range(1, lax.axis_size(axis))]


def short_shards(x_tokens, norm_gain, w_in, short_filter, se_filter, w_out):
    seq, chan = lax.axis_size("seq"), lax.axis_size("chan")
    rows, columns = x_tokens.shape
    tokens, block = rows * seq, w_in.shape[1]
    quarter = block // chan
    wide_rows, wide_columns = 2 * tokens + 8, 3 * quarter // 2

    ahead = lambda weights, times: pl.CostEstimate(
        flops=times * 100 * weights.size * tokens, transcendentals=0, bytes_accessed=times * 8 * weights.size
    )
    x_tokens = call(open_body, struct(x_tokens.shape, BF16), [VMEM], limit=1, cost=ahead(w_in, 2))(x_tokens)
    pieces = gathered(x_tokens, "seq")
    held_in = pltpu.with_memory_space_constraint(w_in, pltpu.VMEM)
    long_taps = call(taps_body, struct((se_filter.shape[0], quarter), F32), [VMEM])(se_filter)
    send, keep = call(
        functools.partial(project_body, seq, quarter),
        (
            struct((2, wide_rows, wide_columns), BF16),
            struct((2, wide_rows, wide_columns), F32),
        ),
        [VMEM] * (seq + 2),
        scratch=[pltpu.VMEM((tokens, columns), F32)],
        limit=10,
    )(*pieces, norm_gain.reshape(1, columns), held_in)
    near = swap(send, "chan", 1)
    relay = call(
        functools.partial(relay_body, 2 * tokens), struct((wide_rows, wide_columns), BF16), [VMEM] * 2, cost=ahead(w_out, 4)
    )(keep, near)
    far = swap(relay, "chan", 2)
    gated = call(
        functools.partial(mix_body, columns * chan), struct((tokens, quarter), BF16), [VMEM] * 5
    )(keep, near, far, short_filter, long_taps)
    pieces = gathered(gated, "seq")
    outputs = w_out.shape[0]
    send, keep = call(
        functools.partial(output_body, seq, quarter),
        (struct((2, tokens // chan, outputs), BF16), struct((2, tokens // chan, outputs), F32)),
        [VMEM] * (seq + 1),
        scratch=[pltpu.VMEM((tokens, outputs), F32)],
        limit=6,
    )(*pieces, pltpu.with_memory_space_constraint(w_out, pltpu.VMEM))
    near = swap(send, "chan", 1)
    relay = call(pass_body, struct((tokens // chan, outputs), BF16), [VMEM] * 2)(keep, near)
    far = swap(relay, "chan", 2)
    return call(close_body, struct((tokens // chan, outputs), BF16), [VMEM] * 3)(keep, near, far)


def from_behind(value, axis, steps):
    count = lax.axis_size(axis)
    leading, last = max(0, -steps), min(count, count - steps)
    return lax.ppermute(value, axis, [(source, source + steps) for source in range(leading, last)])


def mixer(extended, short_taps, long_taps):
    wide = extended.astype(F32)
    row_count = wide.shape[0]
    featured = sum(short_taps[offset] * wide[2 - offset : row_count - offset] for offset in range(3))
    product = featured[:, 1] * featured[:, 2]
    length = product.shape[0]
    filtered = sum(long_taps[offset] * product[6 - offset : length - offset] for offset in range(7))
    return (featured[6:, 0] * filtered).astype(BF16)


def long_shards(x_tokens, norm_gain, w_in, short_filter, se_filter, w_out):
    features = x_tokens.shape[1] * lax.axis_size("chan")
    wide = x_tokens.astype(F32)
    squares = lax.psum(jnp.sum(wide * wide, axis=1, keepdims=True), "chan")
    normed = (wide * lax.rsqrt(squares / features + epsilon) * norm_gain).astype(BF16)
    columns = w_in.shape[1]
    flat_in = w_in.reshape(3 * columns, w_in.shape[2])
    piece = lax.all_gather(normed, "seq", axis=0, tiled=True)
    terms = contract_last(piece, flat_in).reshape(piece.shape[0], 3, columns)
    mine = lax.psum_scatter(terms, "chan", scatter_dimension=0, tiled=True).astype(BF16)
    extended = jnp.concatenate([from_behind(mine[-8:], "chan", 1), mine], axis=0)
    gated = mixer(extended, short_filter, jnp.repeat(se_filter, GROUP, axis=1))
    return contract_last(lax.all_gather(gated, "seq", axis=1, tiled=True), w_out).astype(BF16)


def shards(x_tokens, norm_gain, w_in, short_filter, se_filter, w_out):
    seq, chan = lax.axis_size("seq"), lax.axis_size("chan")
    rows, block = x_tokens.shape[0], w_in.shape[1]
    fits = (
        chan == 4
        and seq == 4
        and rows % 8 == 0
        and rows * seq <= 64
        and block % (2 * LANES * chan) == 0
        and w_out.shape[0] % (PACK * LANES) == 0
        and 2 * w_in.size <= 30 << 20
    )
    return (short_shards if fits else long_shards)(x_tokens, norm_gain, w_in, short_filter, se_filter, w_out)


def solution(mesh):
    placed = (
        P(("parts", "seq"), "chan"),
        P("chan"),
        P(None, "seq", "chan"),
        P(None, None, "seq"),
        P(None, "seq"),
        P("seq", None),
    )
    return jax.shard_map(shards, mesh=mesh, in_specs=placed, out_specs=P(("parts", "chan"), "seq"), check_vma=False)
```

```python
import functools

import jax
import jax.numpy as jnp
from jax import lax
from jax.experimental import pallas as pl
from jax.experimental.pallas import tpu as pltpu
from jax.sharding import PartitionSpec as P

GROUP = 16
epsilon = 1e-06
LANES = 128
PACK = 4
VMEM = pl.BlockSpec(memory_space=pltpu.VMEM)
ANY = pl.BlockSpec(memory_space=pl.ANY)
F32, BF16 = jnp.float32, jnp.bfloat16


def contract_last(left, right):
    return lax.dot_general(left, right, (((1,), (1,)), ((), ())), preferred_element_type=F32)


def spread(rows):
    blank = jnp.zeros_like(rows)
    return [jnp.concatenate([rows if i == q else blank for i in range(PACK)], axis=0) for q in range(PACK)]


def call(body, outs, ins, scratch=(), limit=2, cost=None):
    return pl.pallas_call(
        body,
        out_shape=outs,
        in_specs=ins,
        out_specs=jax.tree.map(lambda _: VMEM, outs),
        scratch_shapes=list(scratch),
        compiler_params=pltpu.CompilerParams(vmem_limit_bytes=limit << 20),
        cost_estimate=cost,
    )


def struct(shape, dtype):
    return jax.ShapeDtypeStruct(shape, dtype)


def open_body(x_ref, o_ref):
    o_ref[...] = x_ref[...]


def taps_body(se, out):
    groups, quarter = se.shape[1], out.shape[1]
    first = lax.axis_index("chan") * (quarter // GROUP)
    row = lax.broadcasted_iota(jnp.int32, (groups, quarter), 0)
    column = lax.broadcasted_iota(jnp.int32, (groups, quarter), 1)
    chosen = jnp.where(row == first + column // GROUP, 1.0, 0.0).astype(BF16)
    rest, total = se[...], 0.0
    for _ in range(3):
        part = rest.astype(BF16)
        total = total + jnp.dot(part, chosen, preferred_element_type=F32)
        rest = rest - part.astype(F32)
    out[...] = total


def high_low(squares):
    high = squares.astype(BF16).astype(F32)
    low = (squares - high).astype(BF16).astype(F32)
    lane = lax.broadcasted_iota(jnp.int32, (8, LANES), 1)
    count = squares.shape[0] // 8
    return jnp.concatenate(
        [jnp.where(lane < LANES // 2, high[8 * i : 8 * i + 8], low[8 * i : 8 * i + 8]) for i in range(count)], axis=1
    )


def from_high_low(packed, count):
    return jnp.concatenate(
        [packed[:, i * LANES : i * LANES + 1] + packed[:, i * LANES + LANES // 2 : i * LANES + LANES // 2 + 1] for i in range(count)],
        axis=0,
    )


def products(w_in, packs, chip, comp):
    c = lax.axis_index("chan")
    half = w_in.shape[1] // (2 * lax.axis_size("chan"))
    total = None
    for other in range(2):
        owner = jnp.bitwise_xor(c, 2 * chip + other)
        for h in range(2):
            start = pl.multiple_of((2 * owner + h) * half, half)
            term = contract_last(w_in[comp, pl.ds(start, half), :], packs[2 * other + h])
            total = term if total is None else total + term
    return total.T


def put(flipped, comp, keep, send):
    rows, half = flipped.shape[0] // 2, flipped.shape[1]
    keep[:rows, comp * half : (comp + 1) * half] = flipped[:rows]
    send[:rows, comp * half : (comp + 1) * half] = flipped[rows:].astype(send.dtype)


def put_squares(packed, keep, send):
    width = packed.shape[1]
    for ref in (keep, send):
        rows, columns = ref.shape
        ref[rows - 8 :, :width] = packed.astype(ref.dtype)
        ref[rows - 8 :, width:] = jnp.zeros((8, columns - width), ref.dtype)


def first_body(seq, *refs):
    pieces, (gain, w_in), (send, keep, scaled, packed), (wide,) = refs[:seq], refs[seq : seq + 2], refs[seq + 2 : seq + 6], refs[seq + 6 :]
    s = lax.axis_index("seq")
    rows = pieces[0].shape[0]
    for hop in range(seq):
        place = pl.multiple_of(jnp.bitwise_xor(s, hop) * rows, rows)
        wide[pl.ds(place, rows), :] = pieces[hop][...].astype(F32)
    tokens = wide[...]
    packed[...] = high_low(jnp.sum(tokens * tokens, axis=1, keepdims=True))
    scaled[...] = (tokens * gain[...]).astype(BF16)
    packs = spread(scaled[...])
    for comp in range(3):
        put(products(w_in, packs, 1, comp), comp, keep, send)
    put_squares(packed[...], keep, send)


def second_body(scaled, w_in, out):
    out[...] = products(w_in, spread(scaled[...]), 0, 0)


def third_body(scaled, w_in, packed, begun, _, send, keep):
    put(begun[...], 0, keep, send)
    packs = spread(scaled[...])
    for comp in (1, 2):
        put(products(w_in, packs, 0, comp), comp, keep, send)
    put_squares(packed[...], keep, send)


def relay_body(rows, keep, got, _, out):
    value = keep[...] + got[...].astype(F32)
    out[:rows, :] = value[:rows].astype(BF16)
    count = rows // 16
    width = count * LANES
    packed = high_low(from_high_low(value[rows:], count))
    out[rows:, :width] = packed.astype(BF16)
    out[rows:, width:] = jnp.zeros((8, value.shape[1] - width), BF16)


def later(value, lag):
    if lag == 0:
        return value
    return jnp.concatenate([jnp.zeros((lag, value.shape[1]), value.dtype), value[: value.shape[0] - lag]], axis=0)


def mix_body(features, keep, near, far, short, long_ref, out):
    c = lax.axis_index("chan")
    value = keep[...] + near[...].astype(F32) + far[...].astype(F32)
    rows = value.shape[0] - 8
    count = rows // 2
    half = value.shape[1] // 3
    squares = from_high_low(value[rows:], count // 8)
    factor = lax.rsqrt(squares / features + epsilon)
    for h in range(2):
        scaled = value[h * count : (h + 1) * count] * factor
        start = pl.multiple_of(c * (2 * half) + h * half, LANES)
        featured = []
        for comp in range(3):
            part = scaled[:, comp * half : (comp + 1) * half]
            taps = [short[lag, comp : comp + 1, pl.ds(start, half)] for lag in range(3)]
            featured.append(sum(taps[lag] * later(part, lag) for lag in range(3)))
        product = featured[1] * featured[2]
        filtered = sum(
            long_ref[lag : lag + 1, h * half : (h + 1) * half] * later(product, lag) for lag in range(long_ref.shape[0])
        )
        out[:, h * half : (h + 1) * half] = (featured[0] * filtered).astype(BF16)


def load_body(seq, quarter, w_out, w_part, sems):
    c = lax.axis_index("chan")
    copies = []
    for source in range(seq):
        start = pl.multiple_of(source * (w_out.shape[1] // seq) + c * quarter, LANES)
        copies.append(pltpu.make_async_copy(w_out.at[:, pl.ds(start, quarter)], w_part.at[source], sems.at[source]))
    for copy in copies:
        copy.start()
    for copy in copies:
        copy.wait()


def output_body(seq, *refs):
    pieces, w_part, (send, keep), (wide,) = refs[:seq], refs[seq], refs[seq + 1 : seq + 3], refs[seq + 3 :]
    s, c = lax.axis_index("seq"), lax.axis_index("chan")
    outputs = w_part.shape[1]
    part = outputs // PACK
    count = pieces[0].shape[0]
    total = None
    for hop in range(seq):
        source = jnp.bitwise_xor(s, hop)
        packs = spread(pieces[hop][...])
        for q in range(PACK):
            term = contract_last(w_part[source, q * part : (q + 1) * part, :], packs[q])
            total = term if total is None else total + term
    flipped = total.T
    for q in range(PACK):
        wide[:, q * part : (q + 1) * part] = flipped[q * count : (q + 1) * count]
    rows = send.shape[1]
    for chip in range(2):
        for other in range(2):
            owner = jnp.bitwise_xor(c, 2 * chip + other)
            value = wide[pl.ds(pl.multiple_of(owner * rows, rows), rows), :]
            if other:
                send[chip] = value.astype(BF16)
            else:
                keep[chip] = value


def pass_body(keep, got, out):
    out[...] = (keep[1] + got[1].astype(F32)).astype(BF16)


def close_body(keep, near, far, out):
    out[...] = (keep[0] + near[0].astype(F32) + far[...].astype(F32)).astype(BF16)


def swap(value, axis, bit):
    return lax.ppermute(value, axis, [(i, i ^ bit) for i in range(lax.axis_size(axis))])


def gathered(value, axis):
    pieces = [value]
    for bit in range(1, lax.axis_size(axis)):
        pieces.append(swap(value, axis, bit))
    return pieces


def short_shards(x_tokens, norm_gain, w_in, short_filter, se_filter, w_out):
    seq, chan = lax.axis_size("seq"), lax.axis_size("chan")
    rows, columns = x_tokens.shape
    tokens, block = rows * seq, w_in.shape[1]
    quarter = block // chan
    wide_rows, wide_columns = 2 * tokens + 8, 3 * quarter // 2

    ahead = lambda weights, times: pl.CostEstimate(
        flops=times * 100 * weights.size * tokens, transcendentals=0, bytes_accessed=times * 8 * weights.size
    )
    x_tokens = call(open_body, struct(x_tokens.shape, BF16), [VMEM], limit=1, cost=ahead(w_in, 2))(x_tokens)
    pieces = gathered(x_tokens, "seq")
    held_in = pltpu.with_memory_space_constraint(w_in, pltpu.VMEM)
    long_taps = call(taps_body, struct((se_filter.shape[0], quarter), F32), [VMEM])(se_filter)
    payload = struct((wide_rows, wide_columns), BF16), struct((wide_rows, wide_columns), F32)
    send, keep, scaled, packed = call(
        functools.partial(first_body, seq),
        (*payload, struct((tokens, columns), BF16), struct((8, tokens // 8 * LANES), F32)),
        [VMEM] * (seq + 2),
        scratch=[pltpu.VMEM((tokens, columns), F32)],
        limit=10,
    )(*pieces, norm_gain.reshape(1, columns), held_in)
    near = swap(send, "chan", 1)
    begun = call(second_body, struct((PACK * tokens, quarter // 2), F32), [VMEM] * 2, limit=3)(scaled, held_in)
    relay = call(
        functools.partial(relay_body, 2 * tokens), payload[0], [VMEM] * 3
    )(keep, near, begun)
    far = swap(relay, "chan", 2)
    send, keep = call(third_body, payload, [VMEM] * 5, limit=3)(scaled, held_in, packed, begun, relay)
    near = swap(send, "chan", 1)
    gated = call(
        functools.partial(mix_body, columns * chan), struct((tokens, quarter), BF16), [VMEM] * 5
    )(keep, near, far, short_filter, long_taps)
    pieces = gathered(gated, "seq")
    outputs = w_out.shape[0]
    w_part = call(
        functools.partial(load_body, seq, quarter),
        pltpu.VMEM((seq, outputs, quarter), BF16),
        [ANY],
        scratch=[pltpu.SemaphoreType.DMA((seq,))],
        limit=1,
    )(pltpu.with_memory_space_constraint(w_out, pltpu.HBM))
    send, keep = call(
        functools.partial(output_body, seq),
        (struct((2, tokens // chan, outputs), BF16), struct((2, tokens // chan, outputs), F32)),
        [VMEM] * (seq + 1),
        scratch=[pltpu.VMEM((tokens, outputs), F32)],
        limit=6,
    )(*pieces, w_part)
    near = swap(send, "chan", 1)
    relay = call(pass_body, struct((tokens // chan, outputs), BF16), [VMEM] * 2)(keep, near)
    far = swap(relay, "chan", 2)
    return call(close_body, struct((tokens // chan, outputs), BF16), [VMEM] * 3)(keep, near, far)


def from_behind(value, axis, steps):
    count = lax.axis_size(axis)
    leading, last = max(0, -steps), min(count, count - steps)
    return lax.ppermute(value, axis, [(source, source + steps) for source in range(leading, last)])


def mixer(extended, short_taps, long_taps):
    wide = extended.astype(F32)
    row_count = wide.shape[0]
    featured = sum(short_taps[offset] * wide[2 - offset : row_count - offset] for offset in range(3))
    product = featured[:, 1] * featured[:, 2]
    length = product.shape[0]
    filtered = sum(long_taps[offset] * product[6 - offset : length - offset] for offset in range(7))
    return (featured[6:, 0] * filtered).astype(BF16)


def long_shards(x_tokens, norm_gain, w_in, short_filter, se_filter, w_out):
    features = x_tokens.shape[1] * lax.axis_size("chan")
    wide = x_tokens.astype(F32)
    squares = lax.psum(jnp.sum(wide * wide, axis=1, keepdims=True), "chan")
    normed = (wide * lax.rsqrt(squares / features + epsilon) * norm_gain).astype(BF16)
    columns = w_in.shape[1]
    flat_in = w_in.reshape(3 * columns, w_in.shape[2])
    piece = lax.all_gather(normed, "seq", axis=0, tiled=True)
    terms = contract_last(piece, flat_in).reshape(piece.shape[0], 3, columns)
    mine = lax.psum_scatter(terms, "chan", scatter_dimension=0, tiled=True).astype(BF16)
    extended = jnp.concatenate([from_behind(mine[-8:], "chan", 1), mine], axis=0)
    gated = mixer(extended, short_filter, jnp.repeat(se_filter, GROUP, axis=1))
    return contract_last(lax.all_gather(gated, "seq", axis=1, tiled=True), w_out).astype(BF16)


def shards(x_tokens, norm_gain, w_in, short_filter, se_filter, w_out):
    seq, chan = lax.axis_size("seq"), lax.axis_size("chan")
    rows, block = x_tokens.shape[0], w_in.shape[1]
    fits = (
        chan == 4
        and seq == 4
        and rows % 8 == 0
        and rows * seq <= 64
        and block % (2 * LANES * chan) == 0
        and w_out.shape[0] % (PACK * LANES) == 0
        and 2 * w_in.size <= 30 << 20
    )
    return (short_shards if fits else long_shards)(x_tokens, norm_gain, w_in, short_filter, se_filter, w_out)


def solution(mesh):
    placed = (
        P(("parts", "seq"), "chan"),
        P("chan"),
        P(None, "seq", "chan"),
        P(None, None, "seq"),
        P(None, "seq"),
        P("seq", None),
    )
    return jax.shard_map(shards, mesh=mesh, in_specs=placed, out_specs=P(("parts", "chan"), "seq"), check_vma=False)
```

```python
import functools

import jax
import jax.numpy as jnp
from jax import lax
from jax.experimental import pallas as pl
from jax.experimental.pallas import tpu as pltpu
from jax.sharding import PartitionSpec as P

GROUP = 16
epsilon = 1e-06
LANES = 128
SPLIT = 1
PACK = 4
VMEM = pl.BlockSpec(memory_space=pltpu.VMEM)
ANY = pl.BlockSpec(memory_space=pl.ANY)
F32, BF16 = jnp.float32, jnp.bfloat16


def contract_last(left, right):
    return lax.dot_general(left, right, (((1,), (1,)), ((), ())), preferred_element_type=F32)


def spread(rows):
    blank = jnp.zeros_like(rows)
    return [jnp.concatenate([rows if i == q else blank for i in range(PACK)], axis=0) for q in range(PACK)]


def call(body, outs, ins, scratch=(), limit=2, cost=None):
    return pl.pallas_call(
        body,
        out_shape=outs,
        in_specs=ins,
        out_specs=jax.tree.map(lambda _: VMEM, outs),
        scratch_shapes=list(scratch),
        compiler_params=pltpu.CompilerParams(vmem_limit_bytes=limit << 20),
        cost_estimate=cost,
    )


def struct(shape, dtype):
    return jax.ShapeDtypeStruct(shape, dtype)


def open_body(x_ref, o_ref):
    o_ref[...] = x_ref[...]


def taps_body(se, out):
    groups, quarter = se.shape[1], out.shape[1]
    first = lax.axis_index("chan") * (quarter // GROUP)
    row = lax.broadcasted_iota(jnp.int32, (groups, quarter), 0)
    column = lax.broadcasted_iota(jnp.int32, (groups, quarter), 1)
    chosen = jnp.where(row == first + column // GROUP, 1.0, 0.0).astype(BF16)
    rest, total = se[...], 0.0
    for _ in range(3):
        part = rest.astype(BF16)
        total = total + jnp.dot(part, chosen, preferred_element_type=F32)
        rest = rest - part.astype(F32)
    out[...] = total


def high_low(squares):
    high = squares.astype(BF16).astype(F32)
    low = (squares - high).astype(BF16).astype(F32)
    lane = lax.broadcasted_iota(jnp.int32, (8, LANES), 1)
    count = squares.shape[0] // 8
    return jnp.concatenate(
        [jnp.where(lane < LANES // 2, high[8 * i : 8 * i + 8], low[8 * i : 8 * i + 8]) for i in range(count)], axis=1
    )


def from_high_low(packed, count):
    return jnp.concatenate(
        [packed[:, i * LANES : i * LANES + 1] + packed[:, i * LANES + LANES // 2 : i * LANES + LANES // 2 + 1] for i in range(count)],
        axis=0,
    )


def products(w_in, packs, chip, comp):
    c = lax.axis_index("chan")
    half = w_in.shape[1] // (2 * lax.axis_size("chan"))
    total = None
    for other in range(2):
        owner = jnp.bitwise_xor(c, 2 * chip + other)
        for h in range(2):
            start = pl.multiple_of((2 * owner + h) * half, half)
            term = contract_last(w_in[comp, pl.ds(start, half), :], packs[2 * other + h])
            total = term if total is None else total + term
    return total.T


def put(flipped, comp, keep, send):
    rows, half = flipped.shape[0] // 2, flipped.shape[1]
    keep[:rows, comp * half : (comp + 1) * half] = flipped[:rows]
    send[:rows, comp * half : (comp + 1) * half] = flipped[rows:].astype(send.dtype)


def put_squares(packed, keep, send):
    width = packed.shape[1]
    for ref in (keep, send):
        rows, columns = ref.shape
        ref[rows - 8 :, :width] = packed.astype(ref.dtype)
        ref[rows - 8 :, width:] = jnp.zeros((8, columns - width), ref.dtype)


def first_body(seq, *refs):
    pieces, (gain, w_in), (send, keep, scaled, packed), (wide,) = refs[:seq], refs[seq : seq + 2], refs[seq + 2 : seq + 6], refs[seq + 6 :]
    s = lax.axis_index("seq")
    rows = pieces[0].shape[0]
    for hop in range(seq):
        place = pl.multiple_of(jnp.bitwise_xor(s, hop) * rows, rows)
        wide[pl.ds(place, rows), :] = pieces[hop][...].astype(F32)
    tokens = wide[...]
    packed[...] = high_low(jnp.sum(tokens * tokens, axis=1, keepdims=True))
    scaled[...] = (tokens * gain[...]).astype(BF16)
    packs = spread(scaled[...])
    for comp in range(3):
        put(products(w_in, packs, 1, comp), comp, keep, send)
    put_squares(packed[...], keep, send)


def second_body(scaled, w_in, out):
    out[...] = products(w_in, spread(scaled[...]), 0, 0)


def third_body(scaled, w_in, packed, begun, _, send, keep):
    put(begun[...], 0, keep, send)
    packs = spread(scaled[...])
    for comp in (1, 2):
        put(products(w_in, packs, 0, comp), comp, keep, send)
    put_squares(packed[...], keep, send)


def relay_body(rows, keep, got, _, out):
    value = keep[...] + got[...].astype(F32)
    out[:rows, :] = value[:rows].astype(BF16)
    count = rows // 16
    width = count * LANES
    packed = high_low(from_high_low(value[rows:], count))
    out[rows:, :width] = packed.astype(BF16)
    out[rows:, width:] = jnp.zeros((8, value.shape[1] - width), BF16)


def later(value, lag):
    if lag == 0:
        return value
    return jnp.concatenate([jnp.zeros((lag, value.shape[1]), value.dtype), value[: value.shape[0] - lag]], axis=0)


def mix_body(features, keep, near, far, short, long_ref, out):
    c = lax.axis_index("chan")
    value = keep[...] + near[...].astype(F32) + far[...].astype(F32)
    rows = value.shape[0] - 8
    count = rows // 2
    half = value.shape[1] // 3
    squares = from_high_low(value[rows:], count // 8)
    factor = lax.rsqrt(squares / features + epsilon)
    for h in range(2):
        scaled = value[h * count : (h + 1) * count] * factor
        start = pl.multiple_of(c * (2 * half) + h * half, LANES)
        featured = []
        for comp in range(3):
            part = scaled[:, comp * half : (comp + 1) * half]
            taps = [short[lag, comp : comp + 1, pl.ds(start, half)] for lag in range(3)]
            featured.append(sum(taps[lag] * later(part, lag) for lag in range(3)))
        product = featured[1] * featured[2]
        filtered = sum(
            long_ref[lag : lag + 1, h * half : (h + 1) * half] * later(product, lag) for lag in range(long_ref.shape[0])
        )
        out[:, h * half : (h + 1) * half] = (featured[0] * filtered).astype(BF16)


def load_body(seq, quarter, hops, w_out, w_part, sems):
    s, c = lax.axis_index("seq"), lax.axis_index("chan")
    copies = []
    for i, hop in enumerate(hops):
        start = pl.multiple_of(jnp.bitwise_xor(s, hop) * (w_out.shape[1] // seq) + c * quarter, LANES)
        copies.append(pltpu.make_async_copy(w_out.at[:, pl.ds(start, quarter)], w_part.at[i], sems.at[i]))
    for copy in copies:
        copy.start()
    for copy in copies:
        copy.wait()


def output_body(seq, split, *refs):
    pieces, parts, (send, keep), (wide,) = refs[:seq], refs[seq : seq + 2], refs[seq + 2 : seq + 4], refs[seq + 4 :]
    c = lax.axis_index("chan")
    outputs = parts[0].shape[1]
    part = outputs // PACK
    count = pieces[0].shape[0]
    total = None
    for hop in range(seq):
        columns = parts[0].at[hop] if hop < split else parts[1].at[hop - split]
        packs = spread(pieces[hop][...])
        for q in range(PACK):
            term = contract_last(columns[q * part : (q + 1) * part, :], packs[q])
            total = term if total is None else total + term
    flipped = total.T
    for q in range(PACK):
        wide[:, q * part : (q + 1) * part] = flipped[q * count : (q + 1) * count]
    rows = send.shape[1]
    for chip in range(2):
        for other in range(2):
            owner = jnp.bitwise_xor(c, 2 * chip + other)
            value = wide[pl.ds(pl.multiple_of(owner * rows, rows), rows), :]
            if other:
                send[chip] = value.astype(BF16)
            else:
                keep[chip] = value


def pass_body(keep, got, out):
    out[...] = (keep[1] + got[1].astype(F32)).astype(BF16)


def close_body(keep, near, far, out):
    out[...] = (keep[0] + near[0].astype(F32) + far[...].astype(F32)).astype(BF16)


def swap(value, axis, bit):
    return lax.ppermute(value, axis, [(i, i ^ bit) for i in range(lax.axis_size(axis))])


def gathered(value, axis):
    pieces = [value]
    for bit in range(1, lax.axis_size(axis)):
        pieces.append(swap(value, axis, bit))
    return pieces


def short_shards(x_tokens, norm_gain, w_in, short_filter, se_filter, w_out):
    seq, chan = lax.axis_size("seq"), lax.axis_size("chan")
    rows, columns = x_tokens.shape
    tokens, block = rows * seq, w_in.shape[1]
    quarter = block // chan
    wide_rows, wide_columns = 2 * tokens + 8, 3 * quarter // 2

    ahead = lambda weights, times: pl.CostEstimate(
        flops=times * 100 * weights.size * tokens, transcendentals=0, bytes_accessed=times * 8 * weights.size
    )
    x_tokens = call(open_body, struct(x_tokens.shape, BF16), [VMEM], limit=1, cost=ahead(w_in, 2))(x_tokens)
    pieces = gathered(x_tokens, "seq")
    held_in = pltpu.with_memory_space_constraint(w_in, pltpu.VMEM)
    long_taps = call(taps_body, struct((se_filter.shape[0], quarter), F32), [VMEM])(se_filter)
    payload = (struct((wide_rows, wide_columns), F32),) * 2
    send, keep, scaled, packed = call(
        functools.partial(first_body, seq),
        (*payload, struct((tokens, columns), BF16), struct((8, tokens // 8 * LANES), F32)),
        [VMEM] * (seq + 2),
        scratch=[pltpu.VMEM((tokens, columns), F32)],
        limit=10,
    )(*pieces, norm_gain.reshape(1, columns), held_in)
    near = swap(send, "chan", 1)
    begun = call(second_body, struct((PACK * tokens, quarter // 2), F32), [VMEM] * 2, limit=3)(scaled, held_in)
    relay = call(
        functools.partial(relay_body, 2 * tokens), struct((wide_rows, wide_columns), BF16), [VMEM] * 3
    )(keep, near, begun)
    far = swap(relay, "chan", 2)
    send, keep = call(third_body, payload, [VMEM] * 5, limit=3)(scaled, held_in, packed, begun, relay)
    near = swap(send, "chan", 1)
    outputs, w_parts = w_out.shape[0], []
    for hops in (range(SPLIT), range(SPLIT, seq)):
        loaded = call(
            functools.partial(load_body, seq, quarter, hops),
            pltpu.VMEM((len(hops), outputs, quarter), BF16),
            [ANY],
            scratch=[pltpu.SemaphoreType.DMA((len(hops),))],
            limit=1,
        )(pltpu.with_memory_space_constraint(w_out, pltpu.HBM))
        w_parts.append(loaded)
    gated = call(
        functools.partial(mix_body, columns * chan), struct((tokens, quarter), BF16), [VMEM] * 5
    )(keep, near, far, short_filter, long_taps)
    pieces = gathered(gated, "seq")
    send, keep = call(
        functools.partial(output_body, seq, SPLIT),
        (struct((2, tokens // chan, outputs), BF16), struct((2, tokens // chan, outputs), F32)),
        [VMEM] * (seq + 2),
        scratch=[pltpu.VMEM((tokens, outputs), F32)],
        limit=6,
    )(*pieces, *w_parts)
    near = swap(send, "chan", 1)
    relay = call(pass_body, struct((tokens // chan, outputs), BF16), [VMEM] * 2)(keep, near)
    far = swap(relay, "chan", 2)
    return call(close_body, struct((tokens // chan, outputs), BF16), [VMEM] * 3)(keep, near, far)


def from_behind(value, axis, steps):
    count = lax.axis_size(axis)
    leading, last = max(0, -steps), min(count, count - steps)
    return lax.ppermute(value, axis, [(source, source + steps) for source in range(leading, last)])


def mixer(extended, short_taps, long_taps):
    wide = extended.astype(F32)
    row_count = wide.shape[0]
    featured = sum(short_taps[offset] * wide[2 - offset : row_count - offset] for offset in range(3))
    product = featured[:, 1] * featured[:, 2]
    length = product.shape[0]
    filtered = sum(long_taps[offset] * product[6 - offset : length - offset] for offset in range(7))
    return (featured[6:, 0] * filtered).astype(BF16)


def long_shards(x_tokens, norm_gain, w_in, short_filter, se_filter, w_out):
    features = x_tokens.shape[1] * lax.axis_size("chan")
    wide = x_tokens.astype(F32)
    squares = lax.psum(jnp.sum(wide * wide, axis=1, keepdims=True), "chan")
    normed = (wide * lax.rsqrt(squares / features + epsilon) * norm_gain).astype(BF16)
    columns = w_in.shape[1]
    flat_in = w_in.reshape(3 * columns, w_in.shape[2])
    piece = lax.all_gather(normed, "seq", axis=0, tiled=True)
    terms = contract_last(piece, flat_in).reshape(piece.shape[0], 3, columns)
    mine = lax.psum_scatter(terms, "chan", scatter_dimension=0, tiled=True).astype(BF16)
    extended = jnp.concatenate([from_behind(mine[-8:], "chan", 1), mine], axis=0)
    gated = mixer(extended, short_filter, jnp.repeat(se_filter, GROUP, axis=1))
    return contract_last(lax.all_gather(gated, "seq", axis=1, tiled=True), w_out).astype(BF16)


def shards(x_tokens, norm_gain, w_in, short_filter, se_filter, w_out):
    seq, chan = lax.axis_size("seq"), lax.axis_size("chan")
    rows, block = x_tokens.shape[0], w_in.shape[1]
    fits = (
        chan == 4
        and seq == 4
        and rows % 8 == 0
        and rows * seq <= 64
        and block % (2 * LANES * chan) == 0
        and w_out.shape[0] % (PACK * LANES) == 0
        and 2 * w_in.size <= 30 << 20
    )
    return (short_shards if fits else long_shards)(x_tokens, norm_gain, w_in, short_filter, se_filter, w_out)


def solution(mesh):
    placed = (
        P(("parts", "seq"), "chan"),
        P("chan"),
        P(None, "seq", "chan"),
        P(None, None, "seq"),
        P(None, "seq"),
        P("seq", None),
    )
    return jax.shard_map(shards, mesh=mesh, in_specs=placed, out_specs=P(("parts", "chan"), "seq"), check_vma=False)
```

```python
import functools

import jax
import jax.numpy as jnp
from jax import lax
from jax.experimental import pallas as pl
from jax.experimental.pallas import tpu as pltpu
from jax.sharding import PartitionSpec as P

GROUP = 16
epsilon = 1e-06
LANES = 128
SPLIT = 1
PACK = 4
VMEM = pl.BlockSpec(memory_space=pltpu.VMEM)
ANY = pl.BlockSpec(memory_space=pl.ANY)
F32, BF16 = jnp.float32, jnp.bfloat16


def contract_last(left, right):
    return lax.dot_general(left, right, (((1,), (1,)), ((), ())), preferred_element_type=F32)


def spread(rows):
    blank = jnp.zeros_like(rows)
    return [jnp.concatenate([rows if i == q else blank for i in range(PACK)], axis=0) for q in range(PACK)]


def call(body, outs, ins, scratch=(), limit=2, cost=None):
    return pl.pallas_call(
        body,
        out_shape=outs,
        in_specs=ins,
        out_specs=jax.tree.map(lambda _: VMEM, outs),
        scratch_shapes=list(scratch),
        compiler_params=pltpu.CompilerParams(vmem_limit_bytes=limit << 20),
        cost_estimate=cost,
    )


def struct(shape, dtype):
    return jax.ShapeDtypeStruct(shape, dtype)


def open_body(x_ref, o_ref):
    o_ref[...] = x_ref[...]


def taps_body(se, out):
    groups, quarter = se.shape[1], out.shape[1]
    first = lax.axis_index("chan") * (quarter // GROUP)
    row = lax.broadcasted_iota(jnp.int32, (groups, quarter), 0)
    column = lax.broadcasted_iota(jnp.int32, (groups, quarter), 1)
    chosen = jnp.where(row == first + column // GROUP, 1.0, 0.0).astype(BF16)
    rest, total = se[...], 0.0
    for _ in range(3):
        part = rest.astype(BF16)
        total = total + jnp.dot(part, chosen, preferred_element_type=F32)
        rest = rest - part.astype(F32)
    out[...] = total


def high_low(squares):
    high = squares.astype(BF16).astype(F32)
    low = (squares - high).astype(BF16).astype(F32)
    lane = lax.broadcasted_iota(jnp.int32, (8, LANES), 1)
    count = squares.shape[0] // 8
    return jnp.concatenate(
        [jnp.where(lane < LANES // 2, high[8 * i : 8 * i + 8], low[8 * i : 8 * i + 8]) for i in range(count)], axis=1
    )


def from_high_low(packed, count):
    return jnp.concatenate(
        [packed[:, i * LANES : i * LANES + 1] + packed[:, i * LANES + LANES // 2 : i * LANES + LANES // 2 + 1] for i in range(count)],
        axis=0,
    )


def doubled(scaled):
    count = scaled.shape[0] // 2
    high, low = spread(scaled[:count]), spread(scaled[count:])
    return [jnp.concatenate(pair, axis=0) for pair in zip(high, low)]


def products(w_in, packs, chip, comp):
    c = lax.axis_index("chan")
    half = w_in.shape[1] // (2 * lax.axis_size("chan"))
    total = None
    for other in range(2):
        owner = jnp.bitwise_xor(c, 2 * chip + other)
        for h in range(2):
            start = pl.multiple_of((2 * owner + h) * half, half)
            term = contract_last(w_in[comp, pl.ds(start, half), :], packs[2 * other + h])
            total = term if total is None else total + term
    flipped = total.T
    count = flipped.shape[0] // 2
    return flipped[:count] + flipped[count:]


def put(flipped, comp, keep, send):
    rows, half = flipped.shape[0] // 2, flipped.shape[1]
    keep[:rows, comp * half : (comp + 1) * half] = flipped[:rows]
    send[:rows, comp * half : (comp + 1) * half] = flipped[rows:].astype(send.dtype)


def put_squares(packed, keep, send):
    width = packed.shape[1]
    for ref in (keep, send):
        rows, columns = ref.shape
        ref[rows - 8 :, :width] = packed.astype(ref.dtype)
        ref[rows - 8 :, width:] = jnp.zeros((8, columns - width), ref.dtype)


def first_body(seq, *refs):
    pieces, (gain, w_in), (send, keep, scaled, packed), (wide,) = refs[:seq], refs[seq : seq + 2], refs[seq + 2 : seq + 6], refs[seq + 6 :]
    s = lax.axis_index("seq")
    rows = pieces[0].shape[0]
    for hop in range(seq):
        place = pl.multiple_of(jnp.bitwise_xor(s, hop) * rows, rows)
        wide[pl.ds(place, rows), :] = pieces[hop][...].astype(F32)
    tokens = wide[...]
    packed[...] = high_low(jnp.sum(tokens * tokens, axis=1, keepdims=True))
    exact = tokens * gain[...]
    high = exact.astype(BF16)
    scaled[: tokens.shape[0]] = high
    scaled[tokens.shape[0] :] = (exact - high.astype(F32)).astype(BF16)
    packs = doubled(scaled[...])
    for comp in range(3):
        put(products(w_in, packs, 1, comp), comp, keep, send)
    put_squares(packed[...], keep, send)


def second_body(scaled, w_in, out):
    out[...] = products(w_in, doubled(scaled[...]), 0, 0)


def third_body(scaled, w_in, packed, begun, _, send, keep):
    put(begun[...], 0, keep, send)
    packs = doubled(scaled[...])
    for comp in (1, 2):
        put(products(w_in, packs, 0, comp), comp, keep, send)
    put_squares(packed[...], keep, send)


def relay_body(rows, keep, got, _, out):
    value = keep[...] + got[...].astype(F32)
    out[:rows, :] = value[:rows].astype(BF16)
    count = rows // 16
    width = count * LANES
    packed = high_low(from_high_low(value[rows:], count))
    out[rows:, :width] = packed.astype(BF16)
    out[rows:, width:] = jnp.zeros((8, value.shape[1] - width), BF16)


def later(value, lag):
    if lag == 0:
        return value
    return jnp.concatenate([jnp.zeros((lag, value.shape[1]), value.dtype), value[: value.shape[0] - lag]], axis=0)


def mix_body(features, keep, near, far, short, long_ref, out):
    c = lax.axis_index("chan")
    value = keep[...] + near[...].astype(F32) + far[...].astype(F32)
    rows = value.shape[0] - 8
    count = rows // 2
    half = value.shape[1] // 3
    squares = from_high_low(value[rows:], count // 8)
    factor = lax.rsqrt(squares / features + epsilon)
    for h in range(2):
        scaled = value[h * count : (h + 1) * count] * factor
        start = pl.multiple_of(c * (2 * half) + h * half, LANES)
        featured = []
        for comp in range(3):
            part = scaled[:, comp * half : (comp + 1) * half]
            taps = [short[lag, comp : comp + 1, pl.ds(start, half)] for lag in range(3)]
            featured.append(sum(taps[lag] * later(part, lag) for lag in range(3)))
        product = featured[1] * featured[2]
        filtered = sum(
            long_ref[lag : lag + 1, h * half : (h + 1) * half] * later(product, lag) for lag in range(long_ref.shape[0])
        )
        out[:, h * half : (h + 1) * half] = (featured[0] * filtered).astype(BF16)


def load_body(seq, quarter, hops, w_out, w_part, sems):
    s, c = lax.axis_index("seq"), lax.axis_index("chan")
    copies = []
    for i, hop in enumerate(hops):
        start = pl.multiple_of(jnp.bitwise_xor(s, hop) * (w_out.shape[1] // seq) + c * quarter, LANES)
        copies.append(pltpu.make_async_copy(w_out.at[:, pl.ds(start, quarter)], w_part.at[i], sems.at[i]))
    for copy in copies:
        copy.start()
    for copy in copies:
        copy.wait()


def output_body(seq, split, *refs):
    pieces, parts, (send, keep), (wide,) = refs[:seq], refs[seq : seq + 2], refs[seq + 2 : seq + 4], refs[seq + 4 :]
    c = lax.axis_index("chan")
    outputs = parts[0].shape[1]
    part = outputs // PACK
    count = pieces[0].shape[0]
    total = None
    for hop in range(seq):
        columns = parts[0].at[hop] if hop < split else parts[1].at[hop - split]
        packs = spread(pieces[hop][...])
        for q in range(PACK):
            term = contract_last(columns[q * part : (q + 1) * part, :], packs[q])
            total = term if total is None else total + term
    flipped = total.T
    for q in range(PACK):
        wide[:, q * part : (q + 1) * part] = flipped[q * count : (q + 1) * count]
    rows = send.shape[1]
    for chip in range(2):
        for other in range(2):
            owner = jnp.bitwise_xor(c, 2 * chip + other)
            value = wide[pl.ds(pl.multiple_of(owner * rows, rows), rows), :]
            if other:
                send[chip] = value.astype(BF16)
            else:
                keep[chip] = value


def pass_body(keep, got, out):
    out[...] = (keep[1] + got[1].astype(F32)).astype(BF16)


def close_body(keep, near, far, out):
    out[...] = (keep[0] + near[0].astype(F32) + far[...].astype(F32)).astype(BF16)


def swap(value, axis, bit):
    return lax.ppermute(value, axis, [(i, i ^ bit) for i in range(lax.axis_size(axis))])


def gathered(value, axis):
    pieces = [value]
    for bit in range(1, lax.axis_size(axis)):
        pieces.append(swap(value, axis, bit))
    return pieces


def short_shards(x_tokens, norm_gain, w_in, short_filter, se_filter, w_out):
    seq, chan = lax.axis_size("seq"), lax.axis_size("chan")
    rows, columns = x_tokens.shape
    tokens, block = rows * seq, w_in.shape[1]
    quarter = block // chan
    wide_rows, wide_columns = 2 * tokens + 8, 3 * quarter // 2

    ahead = lambda weights, times: pl.CostEstimate(
        flops=times * 100 * weights.size * tokens, transcendentals=0, bytes_accessed=times * 8 * weights.size
    )
    x_tokens = call(open_body, struct(x_tokens.shape, BF16), [VMEM], limit=1, cost=ahead(w_in, 2))(x_tokens)
    pieces = gathered(x_tokens, "seq")
    held_in = pltpu.with_memory_space_constraint(w_in, pltpu.VMEM)
    long_taps = call(taps_body, struct((se_filter.shape[0], quarter), F32), [VMEM])(se_filter)
    payload = (struct((wide_rows, wide_columns), F32),) * 2
    send, keep, scaled, packed = call(
        functools.partial(first_body, seq),
        (*payload, struct((2 * tokens, columns), BF16), struct((8, tokens // 8 * LANES), F32)),
        [VMEM] * (seq + 2),
        scratch=[pltpu.VMEM((tokens, columns), F32)],
        limit=14,
    )(*pieces, norm_gain.reshape(1, columns), held_in)
    near = swap(send, "chan", 1)
    begun = call(second_body, struct((PACK * tokens, quarter // 2), F32), [VMEM] * 2, limit=8)(scaled, held_in)
    relay = call(
        functools.partial(relay_body, 2 * tokens), struct((wide_rows, wide_columns), BF16), [VMEM] * 3
    )(keep, near, begun)
    far = swap(relay, "chan", 2)
    send, keep = call(third_body, payload, [VMEM] * 5, limit=8)(scaled, held_in, packed, begun, relay)
    near = swap(send, "chan", 1)
    outputs, w_parts = w_out.shape[0], []
    for hops in (range(SPLIT), range(SPLIT, seq)):
        loaded = call(
            functools.partial(load_body, seq, quarter, hops),
            pltpu.VMEM((len(hops), outputs, quarter), BF16),
            [ANY],
            scratch=[pltpu.SemaphoreType.DMA((len(hops),))],
            limit=1,
        )(pltpu.with_memory_space_constraint(w_out, pltpu.HBM))
        w_parts.append(loaded)
    gated = call(
        functools.partial(mix_body, columns * chan), struct((tokens, quarter), BF16), [VMEM] * 5
    )(keep, near, far, short_filter, long_taps)
    pieces = gathered(gated, "seq")
    send, keep = call(
        functools.partial(output_body, seq, SPLIT),
        (struct((2, tokens // chan, outputs), BF16), struct((2, tokens // chan, outputs), F32)),
        [VMEM] * (seq + 2),
        scratch=[pltpu.VMEM((tokens, outputs), F32)],
        limit=6,
    )(*pieces, *w_parts)
    near = swap(send, "chan", 1)
    relay = call(pass_body, struct((tokens // chan, outputs), BF16), [VMEM] * 2)(keep, near)
    far = swap(relay, "chan", 2)
    return call(close_body, struct((tokens // chan, outputs), BF16), [VMEM] * 3)(keep, near, far)


def from_behind(value, axis, steps):
    count = lax.axis_size(axis)
    leading, last = max(0, -steps), min(count, count - steps)
    return lax.ppermute(value, axis, [(source, source + steps) for source in range(leading, last)])


def mixer(extended, short_taps, long_taps):
    wide = extended.astype(F32)
    row_count = wide.shape[0]
    featured = sum(short_taps[offset] * wide[2 - offset : row_count - offset] for offset in range(3))
    product = featured[:, 1] * featured[:, 2]
    length = product.shape[0]
    filtered = sum(long_taps[offset] * product[6 - offset : length - offset] for offset in range(7))
    return (featured[6:, 0] * filtered).astype(BF16)


def long_shards(x_tokens, norm_gain, w_in, short_filter, se_filter, w_out):
    features = x_tokens.shape[1] * lax.axis_size("chan")
    wide = x_tokens.astype(F32)
    squares = lax.psum(jnp.sum(wide * wide, axis=1, keepdims=True), "chan")
    normed = (wide * lax.rsqrt(squares / features + epsilon) * norm_gain).astype(BF16)
    columns = w_in.shape[1]
    flat_in = w_in.reshape(3 * columns, w_in.shape[2])
    piece = lax.all_gather(normed, "seq", axis=0, tiled=True)
    terms = contract_last(piece, flat_in).reshape(piece.shape[0], 3, columns)
    mine = lax.psum_scatter(terms, "chan", scatter_dimension=0, tiled=True).astype(BF16)
    extended = jnp.concatenate([from_behind(mine[-8:], "chan", 1), mine], axis=0)
    gated = mixer(extended, short_filter, jnp.repeat(se_filter, GROUP, axis=1))
    return contract_last(lax.all_gather(gated, "seq", axis=1, tiled=True), w_out).astype(BF16)


def shards(x_tokens, norm_gain, w_in, short_filter, se_filter, w_out):
    seq, chan = lax.axis_size("seq"), lax.axis_size("chan")
    rows, block = x_tokens.shape[0], w_in.shape[1]
    fits = (
        chan == 4
        and seq == 4
        and rows % 8 == 0
        and rows * seq <= 64
        and block % (2 * LANES * chan) == 0
        and w_out.shape[0] % (PACK * LANES) == 0
        and 2 * w_in.size <= 30 << 20
    )
    return (short_shards if fits else long_shards)(x_tokens, norm_gain, w_in, short_filter, se_filter, w_out)


def solution(mesh):
    placed = (
        P(("parts", "seq"), "chan"),
        P("chan"),
        P(None, "seq", "chan"),
        P(None, None, "seq"),
        P(None, "seq"),
        P("seq", None),
    )
    return jax.shard_map(shards, mesh=mesh, in_specs=placed, out_specs=P(("parts", "chan"), "seq"), check_vma=False)
```
